32 devices in a mesh: dp: 4 (over x, core), seq: 8 (over z, y).
Axes of the slice: x: 2, y: 2, z: 4, core: 2. Of those that a mesh axis runs over, the one named last changes fastest.
Arguments:
- inputs: bfloat16 [2, 4, 1024, 1024], P(None, 'dp', 'seq'), may hold values from -6 to 6
- cotangent: bfloat16 [2, 4, 1024, 1024], P(None, 'dp', 'seq'), may hold values from -6 to 6
- segments: int32 [2, 4, 1024], P(None, 'dp'), may hold values from 0 to 5, never falling along the last dimension, each value on 1 to 768 neighbouring positions
- qkv_weight: bfloat16 [1024, 3072], P(('dp', 'seq')), may hold values from -0.1875 to 0.1875
- out_weight: bfloat16 [1024, 1024], P(('dp', 'seq')), may hold values from -0.75 to 0.75
- up_weight: bfloat16 [1024, 4096], P(('dp', 'seq')), may hold values from -0.1875 to 0.1875
- down_weight: bfloat16 [4096, 1024], P(('dp', 'seq')), may hold values from -0.09375 to 0.09375
- qv_bias: bfloat16 [2, 1024], P(None, ('dp', 'seq')), may hold values from -1.75 to 1.75
- proj_bias: bfloat16 [2, 1024], P(None, ('dp', 'seq')), may hold values from -0.625 to 0.625
- up_bias: bfloat16 [4096], P(('dp', 'seq')), may hold values from -1.75 to 1.75
- norm_gain: bfloat16 [4, 1024], P(None, ('dp', 'seq')), may hold values from 0.5 to 1.5
- norm_bias: bfloat16 [4, 1024], P(None, ('dp', 'seq')), may hold values from -1.75 to 1.75
Outputs:
- layer_out: bfloat16 [2, 4, 1024, 1024], P(None, 'dp', 'seq')
- input_grad: bfloat16 [2, 4, 1024, 1024], P(None, 'dp', 'seq')
- qkv_weight_grad: float32 [1024, 3072], P(('dp', 'seq'))
- out_weight_grad: float32 [1024, 1024], P(('dp', 'seq'))
- up_weight_grad: float32 [1024, 4096], P(('dp', 'seq'))
- down_weight_grad: float32 [4096, 1024], P(('dp', 'seq'))
- qv_bias_grad: float32 [2, 1024], P(None, ('dp', 'seq'))
- proj_bias_grad: float32 [2, 1024], P(None, ('dp', 'seq'))
- up_bias_grad: float32 [4096], P(('dp', 'seq'))
- norm_gain_grad: float32 [4, 1024], P(None, ('dp', 'seq'))
- norm_bias_grad: float32 [4, 1024], P(None, ('dp', 'seq'))
The draws below stay inside these ranges and needn't reach their ends.
Inputs may be any that keep to these rules, and one draw needn't show every extreme that they name: `segments`: along each sequence the document numbers never fall; each of the 6 documents has 1 to 768 positions, and one has exactly 768.
All inputs are finite; a program needn't handle non-finite values.
Results may differ from the reference program's by a relative error of at most 0.012.
Values may be sent and summed in bfloat16 or wider, within the bound.
No kernel may reach another device: no remote copies, remote signals or barrier semaphores. Data moves between devices by JAX's collectives and lax.ppermute only.
A program may use at most 256 MiB of HBM per device.

```python
import math
import jax
import jax.numpy as jnp
import numpy as np
from jax import lax

D = 1024
H = 16
HD = 64
FF = 4096
MB = 2
SEGS = 6
SEQ_LEN = 1024
DOC_MOST = 768
N_DP = 4


def level_of(own_key, shape, split, least, high):
    level = 1.0
    for position, blocks in split:
        draws = jax.random.uniform(jax.random.fold_in(jax.random.fold_in(own_key, 6), position), (blocks,), jnp.float32, least / len(split), high / len(split))
        level = level * jnp.repeat(jnp.exp(draws), shape[position] // blocks).reshape((-1,) + (1,) * (len(shape) - 1 - position))
    return level


def split_up(amount, total, reach, lean):
    weights = [(1 << 20) // math.isqrt(grade ** lean) + 1 for grade in range(2, amount + 1)]
    rest, given = total - reach - (amount - 1), [1] * (amount - 1)
    while rest > 0:
        candidates = [i for i in range(amount - 1) if given[i] < reach]
        pool, left = sum([weights[i] for i in candidates]), rest
        for i in candidates:
            addition = min(reach - given[i], max(1, left * weights[i] // pool), rest)
            given[i] = given[i] + addition
            rest = rest - addition
    return np.array([reach] + given)


def ragged_sizes(stream_key, count, total, bound, skew):
    if count == 2:
        one = jax.random.randint(stream_key, (), max(1, total - bound), min(bound, total - 1) + 1)
        return jnp.stack([one, total - one])
    lengths = jnp.asarray(split_up(count, total, bound, skew), jnp.int32)
    twos = (count - 1) // 2
    giver, receiver = lengths[1:1 + 2 * twos:2], lengths[2:2 + 2 * twos:2]
    slack = jnp.minimum(giver - 1, bound - receiver)
    shifted = jax.random.randint(jax.random.fold_in(stream_key, 1), (twos,), 0, 1 << 20) % (slack + 1)
    lengths = lengths.at[1:1 + 2 * twos:2].set(giver - shifted).at[2:2 + 2 * twos:2].set(receiver + shifted)
    return lengths[jax.random.permutation(jax.random.fold_in(stream_key, 2), count)]


def noise(rng, dims, scale, most, pieces=(), kind=jnp.bfloat16):
    result = scale * jax.random.normal(rng, dims, jnp.float32)
    if pieces:
        result = result * level_of(rng, dims, pieces, -0.22, 0.18)
    return jnp.clip(result, -most, most).astype(kind)


def setup_inputs(seed: int = 0) -> dict:
    seeds = jax.random.split(jax.random.key(seed), 13)
    return {
        "inputs": noise(seeds[0], (MB, N_DP, SEQ_LEN, D), 1.0, 6.0, ((1, 4), (2, 8))),
        "cotangent": noise(seeds[1], (MB, N_DP, SEQ_LEN, D), 1.0, 6.0, ((1, 4), (2, 8))),
        "segments": jax.vmap(lambda own: jnp.searchsorted(jnp.cumsum(ragged_sizes(own, SEGS, SEQ_LEN, DOC_MOST, 2)), jnp.arange(SEQ_LEN), side="right"))(jax.random.split(seeds[2], MB * N_DP)).reshape((MB, N_DP, SEQ_LEN)).astype(jnp.int32),
        "qkv_weight": noise(seeds[3], (D, 3 * D), D ** -0.5, 0.1875, ((0, 32),)),
        "out_weight": noise(seeds[4], (D, D), (D // 16) ** -0.5, 0.75, ((0, 32),)),
        "up_weight": noise(seeds[5], (D, FF), D ** -0.5, 0.1875, ((0, 32),)),
        "down_weight": noise(seeds[6], (FF, D), FF ** -0.5, 0.09375, ((0, 32),)),
        "qv_bias": noise(seeds[7], (2, D), 0.3, 1.75, ((1, 32),)),
        "proj_bias": noise(seeds[8], (2, D), 0.1, 0.625, ((1, 32),)),
        "up_bias": noise(seeds[9], (FF,), 0.3, 1.75, ((0, 32),)),
        "norm_gain": jnp.clip(1.0 + 0.1 * jax.random.normal(seeds[10], (4, D), jnp.float32), 0.5, 1.5).astype(jnp.bfloat16),
        "norm_bias": noise(seeds[11], (4, D), 0.3, 1.75, ((1, 32),)),
    }


EPS = 1e-05
NEG = -1e+30
RELAX = 32.0
HIGH = lax.Precision.HIGHEST

@jax.custom_vjp
def low(v):
    return lax.optimization_barrier(v.astype(jnp.bfloat16)).astype(jnp.float32)

@jax.custom_vjp
def low_back(v):
    return v

def low_keep(v):
    return (low(v), None)

def low_pass(kept, grad):
    return (grad,)

def back_keep(v):
    return (v, None)

def back_low(kept, grad):
    return (low(grad),)
low.defvjp(low_keep, low_pass)
low_back.defvjp(back_keep, back_low)

def layer_norm(value, gain, shift):
    centre = lax.optimization_barrier(jnp.mean(value, -1, keepdims=True))
    centred = value - centre
    spread = lax.optimization_barrier(jnp.mean(centred * centred, -1, keepdims=True))
    return centred * lax.rsqrt(spread + EPS) * gain + shift

def attend(query, keys, values, documents):
    length = query.shape[0]
    block = min(512, length)
    shrink = HD ** (-0.5) / RELAX
    places = jnp.arange(length, dtype=jnp.int32)

    def one_block(index):
        first = index * block
        query_part = lax.dynamic_slice_in_dim(query, first, block, 0)
        docs_part = lax.dynamic_slice_in_dim(documents, first, block, 0)
        places_part = first + jnp.arange(block, dtype=jnp.int32)
        scores = low_back(jnp.einsum('rhd,khd->hrk', query_part * shrink, keys, precision=HIGH) * RELAX)
        visible = (places_part[:, None] >= places[None, :]) & (docs_part[:, None] == documents[None, :])
        scores = jnp.where(visible[None], scores, NEG)
        peak = lax.optimization_barrier(jnp.max(scores, -1, keepdims=True))
        logsum = peak + jnp.log(lax.optimization_barrier(jnp.sum(jnp.exp(scores - peak), -1, keepdims=True)))
        soft = low(jnp.exp(scores - logsum))
        return jnp.einsum('hrk,khd->rhd', soft, values, precision=HIGH)
    blocks = lax.map(jax.checkpoint(one_block), jnp.arange(length // block, dtype=jnp.int32))
    return blocks.reshape(length, H * HD)

def layer(tokens, params, documents):
    w_qkv, w_out, w_up, w_down, bias_qv, bias_proj, bias_up, gains, shifts = params
    normed = low(layer_norm(tokens, gains[0], shifts[0]))
    mixed = jnp.dot(normed, w_qkv, precision=HIGH)
    query = low(low_back(mixed[:, :D] + bias_qv[0]))
    keys = low(low_back(mixed[:, D:2 * D]))
    values = low(low_back(mixed[:, 2 * D:] + bias_qv[1]))
    length = tokens.shape[0]
    attended = attend(query.reshape(length, H, HD), keys.reshape(length, H, HD), values.reshape(length, H, HD), documents)
    attended = low(low_back(attended))
    branch = low_back(jnp.dot(attended, w_out, precision=HIGH)) + bias_proj[0]
    middle = tokens + layer_norm(branch, gains[1], shifts[1])
    second = low(layer_norm(middle, gains[2], shifts[2]))
    hidden = low_back(jnp.dot(second, w_up, precision=HIGH)) + bias_up
    active = low(jax.nn.gelu(hidden))
    down = low_back(jnp.dot(active, w_down, precision=HIGH)) + bias_proj[1]
    return middle + layer_norm(down, gains[3], shifts[3])

def reference(inputs, cotangent, segments, qkv_weight, out_weight, up_weight, down_weight, qv_bias, proj_bias, up_bias, norm_gain, norm_bias):
    params = (qkv_weight.astype(jnp.float32), out_weight.astype(jnp.float32), up_weight.astype(jnp.float32), down_weight.astype(jnp.float32), qv_bias.astype(jnp.float32), proj_bias.astype(jnp.float32), up_bias.astype(jnp.float32), norm_gain.astype(jnp.float32), norm_bias.astype(jnp.float32))
    sequences = inputs.reshape(MB * N_DP, SEQ_LEN, D).astype(jnp.float32)
    documents = segments.reshape(MB * N_DP, SEQ_LEN)

    def forward(sequences, params):

        def one_layer(tokens, docs):
            return layer(tokens, params, docs)
        checked = jax.checkpoint(one_layer)

        def step(carry, item):
            return (carry, checked(item[0], item[1]))
        unused, outputs = lax.scan(step, jnp.zeros((), jnp.float32), (sequences, documents))
        return outputs
    outputs, pullback = jax.vjp(forward, sequences, params)
    grad_in = cotangent.reshape(MB * N_DP, SEQ_LEN, D).astype(jnp.float32)
    grad_tokens, grad_params = pullback(grad_in)
    layer_out = outputs.reshape(MB, N_DP, SEQ_LEN, D).astype(jnp.bfloat16)
    input_grad = grad_tokens.reshape(MB, N_DP, SEQ_LEN, D).astype(jnp.bfloat16)
    return (layer_out, input_grad, grad_params[0], grad_params[1], grad_params[2], grad_params[3], grad_params[4], grad_params[5], grad_params[6], grad_params[7], grad_params[8])
```

```python
import functools

import jax
import jax.numpy as jnp
from jax import lax
from jax.experimental import pallas as pl
from jax.experimental.pallas import tpu as pltpu
from jax.sharding import PartitionSpec as P

D = 1024
H = 16
HD = 64
MB = 2

EPS = 1e-05
NEG = -1e30
SHRINK = HD ** (-0.5)
BF16 = jnp.bfloat16
F32 = jnp.float32
C0 = 0.7978845608028654
C1 = 0.044715


def dot(a, b, dims):
    return lax.dot_general(a, b, (dims, ((), ())), preferred_element_type=F32)


def head_mask(x, h, heads):
    if heads == 1:
        return x
    lane = lax.broadcasted_iota(jnp.int32, x.shape, 1)
    return jnp.where(lane // HD == h, x, jnp.zeros_like(x))


def transpose(x):
    return x.astype(F32).T


def attend_forward_kernel(
    heads, blk, pos_ref, lo_ref, start_ref, q_ref, k_ref, v_ref, o_ref, ot_ref, lse_ref, qn, kn, vt
):
    slots, rows = q_ref.shape[0], q_ref.shape[2]
    length = qn.shape[0]
    batch = pl.program_id(0)
    for j in range(slots):
        at = pl.multiple_of(pos_ref[j] * rows, rows)
        qn[pl.ds(at, rows), :] = q_ref[j, 0]
        kn[pl.ds(at, rows), :] = k_ref[j, 0]
        vt[:, pl.ds(at, rows)] = transpose(v_ref[j, 0]).astype(BF16)
    for i in range(length // blk):
        start = start_ref[0, 0:1, i * blk : (i + 1) * blk]
        qpos = i * blk + lax.broadcasted_iota(jnp.int32, (blk, blk), 1)
        base = lax.broadcasted_iota(jnp.int32, (blk, blk), 0)
        for h in range(heads):
            qh = head_mask(qn[i * blk : (i + 1) * blk, :], h, heads) * BF16(SHRINK)

            def step(j, carry, qh=qh, start=start, qpos=qpos, base=base, h=h):
                peak, total, acc = carry
                first = pl.multiple_of(j * blk, blk)
                st = dot(kn[pl.ds(first, blk), :], qh, ((1,), (1,)))
                kpos = base + first
                st = jnp.where((kpos >= start) & (kpos <= qpos), st, NEG)
                new = jnp.maximum(peak, jnp.max(st, 0, keepdims=True))
                pt = jnp.exp(st - new)
                keep = jnp.exp(peak - new)
                total = total * keep + jnp.sum(pt, 0, keepdims=True)
                vh = vt[h * HD : (h + 1) * HD, pl.ds(first, blk)]
                acc = acc * keep + dot(vh, pt.astype(BF16), ((1,), (0,)))
                return (new, total, acc)

            init = (
                jnp.full((1, blk), NEG, F32),
                jnp.zeros((1, blk), F32),
                jnp.zeros((HD, blk), F32),
            )
            peak, total, acc = lax.fori_loop(lo_ref[batch, i], i + 1, step, init)
            lse_ref[0, h : h + 1, i * blk : (i + 1) * blk] = peak + jnp.log(total)
            ot_ref[0, h * HD : (h + 1) * HD, i * blk : (i + 1) * blk] = acc / total
    for j in range(slots):
        o_ref[j, 0] = ot_ref[0, :, j * rows : (j + 1) * rows].T.astype(BF16)


def attend_backward_kernel(
    heads,
    blk,
    pos_ref,
    hi_ref,
    start_ref,
    q_ref,
    k_ref,
    v_ref,
    ga_ref,
    ot_ref,
    lse_ref,
    dq_ref,
    dk_ref,
    dv_ref,
    qn,
    kn,
    vn,
    gan,
    kt,
    dqt,
    dkn,
    dvn,
    delta,
):
    slots, rows = q_ref.shape[0], q_ref.shape[2]
    length = qn.shape[0]
    batch = pl.program_id(0)
    for j in range(slots):
        at = pl.multiple_of(pos_ref[j] * rows, rows)
        qn[pl.ds(at, rows), :] = q_ref[j, 0] * BF16(SHRINK)
        kn[pl.ds(at, rows), :] = k_ref[j, 0]
        vn[pl.ds(at, rows), :] = v_ref[j, 0]
        kt[:, pl.ds(at, rows)] = transpose(k_ref[j, 0]).astype(BF16)
        ga = ga_ref[j, 0]
        gan[j * rows : (j + 1) * rows, :] = ga
        prod = transpose(ga) * ot_ref[0, :, j * rows : (j + 1) * rows]
        for h in range(heads):
            delta[h : h + 1, j * rows : (j + 1) * rows] = jnp.sum(
                prod[h * HD : (h + 1) * HD], 0, keepdims=True
            )
    dqt[...] = jnp.zeros_like(dqt)
    for j in range(length // blk):
        key = kn[j * blk : (j + 1) * blk, :]
        value = vn[j * blk : (j + 1) * blk, :]
        kpos = j * blk + lax.broadcasted_iota(jnp.int32, (blk, blk), 0)
        base = lax.broadcasted_iota(jnp.int32, (blk, blk), 1)

        def step(i, carry, key=key, value=value, kpos=kpos, base=base, j=j):
            dk, dv = carry
            first = pl.multiple_of(i * blk, blk)
            cols = pl.ds(first, blk)
            start = start_ref[0, 0:1, cols]
            visible = (kpos >= start) & (kpos <= base + first)
            qall = qn[cols, :]
            gall = gan[cols, :]
            for h in range(heads):
                qh = head_mask(qall, h, heads)
                gh = head_mask(gall, h, heads)
                st = dot(key, qh, ((1,), (1,)))
                pt = jnp.where(visible, jnp.exp(st - lse_ref[0, h : h + 1, cols]), 0.0)
                dpt = dot(value, gh, ((1,), (1,)))
                dst = (pt * (dpt - delta[h : h + 1, cols])).astype(BF16)
                dv = dv + dot(pt.astype(BF16), gh, ((1,), (0,)))
                dk = dk + dot(dst, qh, ((1,), (0,)))
                part = dot(kt[h * HD : (h + 1) * HD, j * blk : (j + 1) * blk], dst, ((1,), (0,)))
                dqt[h * HD : (h + 1) * HD, cols] = dqt[h * HD : (h + 1) * HD, cols] + part
            return (dk, dv)

        zero = jnp.zeros((blk, heads * HD), F32)
        dk, dv = lax.fori_loop(j, hi_ref[batch, j] + 1, step, (zero, zero))
        dkn[j * blk : (j + 1) * blk, :] = dk.astype(BF16)
        dvn[j * blk : (j + 1) * blk, :] = dv.astype(BF16)
    for j in range(slots):
        at = pl.multiple_of(pos_ref[j] * rows, rows)
        dq_ref[j, 0] = ((dqt[:, pl.ds(at, rows)] * SHRINK).T).astype(BF16)
        dk_ref[j, 0] = dkn[pl.ds(at, rows), :]
        dv_ref[j, 0] = dvn[pl.ds(at, rows), :]


def attention_specs(slots, rows, lanes, length, heads):
    piece = pl.BlockSpec((slots, 1, rows, lanes), lambda b, *_: (0, b, 0, 0))
    starts = pl.BlockSpec((1, 1, length), lambda b, *_: (b, 0, 0))
    turned = pl.BlockSpec((1, lanes, length), lambda b, *_: (b, 0, 0))
    sums = pl.BlockSpec((1, heads, length), lambda b, *_: (b, 0, 0))
    return piece, starts, turned, sums


def attend_forward(pos, lo, start, q, k, v, blk):
    slots, batches, rows, lanes = q.shape
    length, heads = slots * rows, lanes // HD
    piece, starts, turned, sums = attention_specs(slots, rows, lanes, length, heads)
    pairs = batches * heads * length * length
    return pl.pallas_call(
        functools.partial(attend_forward_kernel, heads, blk),
        out_shape=(
            jax.ShapeDtypeStruct(q.shape, BF16),
            jax.ShapeDtypeStruct((batches, lanes, length), F32),
            jax.ShapeDtypeStruct((batches, heads, length), F32),
        ),
        grid_spec=pltpu.PrefetchScalarGridSpec(
            num_scalar_prefetch=2,
            grid=(batches,),
            in_specs=[starts, piece, piece, piece],
            out_specs=[piece, turned, sums],
            scratch_shapes=[
                pltpu.VMEM((length, lanes), BF16),
                pltpu.VMEM((length, lanes), BF16),
                pltpu.VMEM((lanes, length), BF16),
            ],
        ),
        cost_estimate=pl.CostEstimate(
            flops=pairs * 4 * HD, bytes_accessed=q.size * 16, transcendentals=pairs
        ),
        name="attend_forward",
    )(pos, lo, start, q, k, v)


def attend_backward(pos, hi, start, q, k, v, ga, ot, lse, blk):
    slots, batches, rows, lanes = q.shape
    length, heads = slots * rows, lanes // HD
    piece, starts, turned, sums = attention_specs(slots, rows, lanes, length, heads)
    pairs = batches * heads * length * length
    return pl.pallas_call(
        functools.partial(attend_backward_kernel, heads, blk),
        out_shape=(jax.ShapeDtypeStruct(q.shape, BF16),) * 3,
        grid_spec=pltpu.PrefetchScalarGridSpec(
            num_scalar_prefetch=2,
            grid=(batches,),
            in_specs=[starts, piece, piece, piece, piece, turned, sums],
            out_specs=[piece, piece, piece],
            scratch_shapes=[pltpu.VMEM((length, lanes), BF16)] * 4
            + [
                pltpu.VMEM((lanes, length), BF16),
                pltpu.VMEM((lanes, length), F32),
                pltpu.VMEM((length, lanes), BF16),
                pltpu.VMEM((length, lanes), BF16),
                pltpu.VMEM((heads, length), F32),
            ],
        ),
        cost_estimate=pl.CostEstimate(
            flops=pairs * 10 * HD, bytes_accessed=q.size * 20, transcendentals=pairs
        ),
        name="attend_backward",
    )(pos, hi, start, q, k, v, ga, ot, lse)


def gelu_parts(h):
    t = jnp.tanh(C0 * (h + C1 * (h * h * h)))
    return t, 0.5 * h * (1.0 + t)


def gelu_slope(h):
    t = jnp.tanh(C0 * (h + C1 * (h * h * h)))
    return 0.5 * (1.0 + t) + 0.5 * h * (1.0 - t * t) * (C0 * (1.0 + 3.0 * C1 * (h * h)))


def gelu_forward_kernel(order_ref, h_ref, a_ref):
    width = 128

    def step(j, carry):
        src = pl.multiple_of(order_ref[j] * width, width)
        dst = pl.multiple_of(j * width, width)
        a_ref[:, pl.ds(dst, width)] = gelu_parts(h_ref[:, pl.ds(src, width)])[1].astype(BF16)
        return carry

    lax.fori_loop(0, h_ref.shape[1] // width, step, 0)


def gelu_backward_kernel(order_ref, h_ref, ga_ref, gh_ref, sum_ref):
    width = 128

    @pl.when(pl.program_id(0) == 0)
    def _():
        sum_ref[...] = jnp.zeros_like(sum_ref)

    def step(j, carry):
        dst = pl.multiple_of(order_ref[j] * width, width)
        src = pl.multiple_of(j * width, width)
        g = ga_ref[:, pl.ds(src, width)] * gelu_slope(h_ref[:, pl.ds(dst, width)])
        gh_ref[:, pl.ds(dst, width)] = g.astype(BF16)
        sum_ref[:, pl.ds(dst, width)] = sum_ref[:, pl.ds(dst, width)] + jnp.sum(
            g, 0, keepdims=True
        )
        return carry

    lax.fori_loop(0, h_ref.shape[1] // width, step, 0)


def chunk_order(order, height):
    many = height // 128
    return (order[:, None] * many + jnp.arange(many, dtype=jnp.int32)[None]).reshape(-1)


def gelu_forward(hidden, order, height):
    rows, width = hidden.shape
    if height % 128:
        act = gelu_parts(hidden)[1].astype(BF16).reshape(rows, -1, height)
        return jnp.take(act, order, axis=1).reshape(rows, width)
    tall = min(rows, 64)
    spec = pl.BlockSpec((tall, width), lambda i, *_: (i, 0))
    return pl.pallas_call(
        gelu_forward_kernel,
        out_shape=jax.ShapeDtypeStruct((rows, width), BF16),
        grid_spec=pltpu.PrefetchScalarGridSpec(
            num_scalar_prefetch=1, grid=(rows // tall,), in_specs=[spec], out_specs=spec
        ),
        cost_estimate=pl.CostEstimate(
            flops=rows * width * 10, bytes_accessed=rows * width * 6, transcendentals=rows * width
        ),
        name="gelu_forward",
    )(chunk_order(order, height), hidden)


def gelu_backward(hidden, grad, order, height):
    rows, width = hidden.shape
    if height % 128:
        back = jnp.argsort(order)
        grad = jnp.take(grad.reshape(rows, -1, height), back, axis=1).reshape(rows, width)
        grad = grad * gelu_slope(hidden)
        return grad.astype(BF16), jnp.sum(grad, 0, keepdims=True)
    tall = min(rows, 64)
    spec = pl.BlockSpec((tall, width), lambda i, *_: (i, 0))
    return pl.pallas_call(
        gelu_backward_kernel,
        out_shape=(
            jax.ShapeDtypeStruct((rows, width), BF16),
            jax.ShapeDtypeStruct((1, width), F32),
        ),
        grid_spec=pltpu.PrefetchScalarGridSpec(
            num_scalar_prefetch=1,
            grid=(rows // tall,),
            in_specs=[spec, spec],
            out_specs=[spec, pl.BlockSpec((1, width), lambda i, *_: (0, 0))],
        ),
        cost_estimate=pl.CostEstimate(
            flops=rows * width * 20, bytes_accessed=rows * width * 10, transcendentals=rows * width
        ),
        name="gelu_backward",
    )(chunk_order(order, height), hidden, grad)


class Net:
    def __init__(self, n_dp, n_seq):
        self.n_dp, self.n_seq = n_dp, n_seq
        self.nx, self.nz = n_dp // 2, n_seq // 2
        self.core = [(i, i ^ 1) for i in range(n_dp)]
        self.y = [(i, i ^ 1) for i in range(n_seq)]
        self.x_next = [(i, (i + 2) % n_dp) for i in range(n_dp)]
        self.z_next = [(i, (i + 2) % n_seq) for i in range(n_seq)]
        self.x_prev = [(b, a) for a, b in self.x_next]
        self.z_prev = [(b, a) for a, b in self.z_next]
        self.d = lax.axis_index("dp")
        self.s = lax.axis_index("seq")

    def seq_order(self):
        k = jnp.arange(self.nz, dtype=jnp.int32)[:, None]
        yr = jnp.arange(2, dtype=jnp.int32)[None, :]
        z = lax.rem(self.s // 2 - k + self.nz, self.nz)
        return (z * 2 + jnp.bitwise_xor(lax.rem(self.s, 2), yr)).reshape(-1).astype(jnp.int32)

    def all_order(self):
        j = jnp.arange(self.nx, dtype=jnp.int32)[None, :]
        c = jnp.arange(2, dtype=jnp.int32)[:, None]
        x = lax.rem(self.d // 2 - j + self.nx, self.nx)
        dp = x * 2 + jnp.bitwise_xor(lax.rem(self.d, 2), c)
        seq = self.seq_order().reshape(self.nz, 2)
        return (dp[None, :, :, None] * self.n_seq + seq[:, None, None, :]).reshape(-1)

    def gather_seq(self, a):
        ring = [a]
        for _ in range(self.nz - 1):
            ring.append(lax.ppermute(ring[-1], "seq", self.z_next))
        slots = []
        for piece in ring:
            slots += [piece, lax.ppermute(piece, "seq", self.y)]
        return slots

    def gather_all(self, a):
        pieces = []
        slots = self.gather_seq(a)
        for k in range(self.nz):
            pair = jnp.concatenate(slots[2 * k : 2 * k + 2], 0)
            ring = [pair]
            for _ in range(self.nx - 1):
                ring.append(lax.ppermute(ring[-1], "dp", self.x_next))
            quad = jnp.concatenate(ring, 0)
            pieces += [quad, lax.ppermute(quad, "dp", self.core)]
        return pieces

    def scatter_all(self, left, right):
        step = left.shape[1] // (2 * self.nz)
        height = step // (2 * self.nx)
        done = None
        for k in reversed(range(self.nz)):
            at = 2 * k * step
            away = dot(left[:, at + step : at + 2 * step], right, ((0,), (0,))).astype(BF16)
            own = dot(left[:, at : at + step], right, ((0,), (0,)))
            own = own + lax.ppermute(away, "dp", self.core).astype(F32)
            own = own.reshape(self.nx, 2 * height, -1)
            total = own[self.nx - 1]
            for j in reversed(range(self.nx - 1)):
                total = own[j] + lax.ppermute(total.astype(BF16), "dp", self.x_prev).astype(F32)
            total = total[:height] + lax.ppermute(
                total[height:].astype(BF16), "seq", self.y
            ).astype(F32)
            if done is not None:
                total = total + lax.ppermute(done.astype(BF16), "seq", self.z_prev).astype(F32)
            done = total
        return done

    def scatter_seq(self, slots):
        done = None
        for k in reversed(range(self.nz)):
            total = slots[2 * k] + lax.ppermute(
                slots[2 * k + 1].astype(BF16), "seq", self.y
            ).astype(F32)
            if done is not None:
                total = total + lax.ppermute(done.astype(BF16), "seq", self.z_prev).astype(F32)
            done = total
        return done

    def gather_small(self, a):
        n_dp, n_seq = self.n_dp, self.n_seq
        rows = [a]
        for t in range(1, n_seq):
            rows.append(lax.ppermute(a, "seq", [(i, (i + t) % n_seq) for i in range(n_seq)]))
        group = jnp.stack(rows)
        groups = [group]
        for u in range(1, n_dp):
            groups.append(lax.ppermute(group, "dp", [(i, (i + u) % n_dp) for i in range(n_dp)]))
        mixed = jnp.concatenate(groups, 0)
        u = jnp.arange(n_dp, dtype=jnp.int32)[:, None]
        t = jnp.arange(n_seq, dtype=jnp.int32)[None, :]
        order = lax.rem(self.d - u + n_dp, n_dp) * n_seq + lax.rem(self.s - t + n_seq, n_seq)
        place = jnp.arange(n_dp * n_seq, dtype=jnp.int32)[:, None] == order.reshape(1, -1)
        return dot(place.astype(BF16), mixed, ((1,), (0,)))


def swap_all(a, axis_name):
    return lax.all_to_all(a, axis_name, 0, 0, tiled=True)


def ln_stats(value):
    centre = jnp.mean(value, -1, keepdims=True)
    centred = value - centre
    spread = jnp.mean(centred * centred, -1, keepdims=True)
    root = lax.rsqrt(spread + EPS)
    return centred * root, root


def ln_back(unit, root, gain, grad):
    c = grad * gain
    return root * (
        c
        - jnp.mean(c, -1, keepdims=True)
        - unit * jnp.mean(c * unit, -1, keepdims=True)
    )


def body(
    n_dp,
    n_seq,
    inputs,
    cotangent,
    segments,
    qkv_weight,
    out_weight,
    up_weight,
    down_weight,
    qv_bias,
    proj_bias,
    up_bias,
    norm_gain,
    norm_bias,
):
    net = Net(n_dp, n_seq)
    devices = n_dp * n_seq
    height = inputs.shape[2]
    length = segments.shape[2]
    count = MB * height
    heads = H // n_seq
    lanes = heads * HD
    blk = min(256, length)
    order = net.all_order()
    pos = net.seq_order()
    tokens16 = inputs.reshape(count, D)
    tokens = tokens16.astype(F32)

    token_slots = net.gather_seq(tokens16)
    small = jnp.concatenate(
        [a.reshape(-1) for a in (qv_bias, proj_bias, up_bias, norm_gain, norm_bias)]
    )
    small = net.gather_small(small)
    share = D // devices
    wide = up_bias.shape[0]

    def unpack(first, many):
        part = small[:, first : first + many * share].reshape(devices, many, share)
        return part.transpose(1, 0, 2).reshape(many, D)

    bias_qv = unpack(0, 2)
    bias_proj = unpack(2 * share, 2)
    bias_up = small[:, 4 * share : 4 * share + wide].reshape(1, devices * wide)
    gains = unpack(4 * share + wide, 4)
    shifts = unpack(8 * share + wide, 4)

    rows_out, rows_qkv = out_weight.shape[0], qkv_weight.shape[0]
    mine = qkv_weight.reshape(rows_qkv, 3, n_seq, lanes).transpose(2, 0, 1, 3)
    mine = swap_all(mine.reshape(n_seq, rows_qkv, 3 * lanes), "seq")
    mine = mine.reshape(n_seq * rows_qkv, 3 * lanes)
    w_heads = jnp.zeros((D, 3 * lanes), BF16)
    for u in range(n_dp):
        part = mine
        if u:
            part = lax.ppermute(mine, "dp", [(i, (i + u) % n_dp) for i in range(n_dp)])
        at = lax.rem(net.d - u + n_dp, n_dp) * (n_seq * rows_qkv)
        w_heads = lax.dynamic_update_slice(w_heads, part, (at, jnp.int32(0)))

    first_pieces = net.gather_all(jnp.concatenate([out_weight, up_weight], 1))
    w_out = jnp.concatenate([p[:, :D] for p in first_pieces], 0)
    w_up = jnp.concatenate([p[:, D:] for p in first_pieces], 0)
    w_down = jnp.concatenate(net.gather_all(down_weight), 0)

    source = (order[:, None] * rows_out + jnp.arange(rows_out, dtype=jnp.int32)[None]).reshape(1, D)
    shuffle = (jnp.arange(D, dtype=jnp.int32)[:, None] == source).astype(BF16)

    docs = segments[:, 0]
    start = jnp.sum((docs[:, None, :] < docs[:, :, None]).astype(jnp.int32), -1)
    low = start[:, ::blk] // blk
    last = docs[:, blk - 1 :: blk]
    high = (jnp.sum((docs[:, None, :] <= last[:, :, None]).astype(jnp.int32), -1) - 1) // blk
    start = start[:, None, :]

    at = net.s * lanes
    bias_q = lax.dynamic_slice(bias_qv, (jnp.int32(0), at), (1, lanes))
    bias_v = lax.dynamic_slice(bias_qv, (jnp.int32(1), at), (1, lanes))
    bias_heads = jnp.concatenate([bias_q, jnp.zeros_like(bias_q), bias_v], 1)
    normed, mixed, units = [], [], []
    for piece in token_slots:
        unit, _ = ln_stats(piece.astype(F32))
        line = (unit * gains[0] + shifts[0]).astype(BF16)
        normed.append(line)
        units.append(unit)
        mixed.append((dot(line, w_heads, ((1,), (0,))) + bias_heads).astype(BF16))

    def part_of(k):
        parts = [m[:, k * lanes : (k + 1) * lanes] for m in mixed]
        return jnp.stack(parts).reshape(n_seq, MB, height, lanes)

    query, keys, values = part_of(0), part_of(1), part_of(2)
    attended_heads, turned, logsum = attend_forward(pos, low, start, query, keys, values, blk)
    attended = swap_all(attended_heads, "seq").reshape(n_seq, count, lanes)
    attended = attended.transpose(1, 0, 2).reshape(count, D)
    attended = dot(attended, shuffle, ((1,), (0,))).astype(BF16)

    branch = dot(attended, w_out, ((1,), (0,))) + bias_proj[0]
    unit_one, root_one = ln_stats(branch)
    middle = tokens + (unit_one * gains[1] + shifts[1])
    unit_two, root_two = ln_stats(middle)
    second = (unit_two * gains[2] + shifts[2]).astype(BF16)
    second = dot(second, shuffle, ((1,), (0,))).astype(BF16)
    hidden = dot(second, w_up, ((1,), (0,))) + bias_up
    active = gelu_forward(hidden, order, down_weight.shape[0])
    down = dot(active, w_down, ((1,), (0,))) + bias_proj[1]
    unit_three, root_three = ln_stats(down)
    layer_out = (middle + (unit_three * gains[3] + shifts[3])).astype(BF16)

    dy = cotangent.reshape(count, D).astype(F32)
    grad_gain_three = jnp.sum(dy * unit_three, 0)
    grad_shift_three = jnp.sum(dy, 0)
    grad_down32 = ln_back(unit_three, root_three, gains[3], dy)
    grad_bias_down = jnp.sum(grad_down32, 0)
    grad_down = grad_down32.astype(BF16)
    grad_active = dot(grad_down, w_down, ((1,), (1,)))
    shard_down = net.scatter_all(active, grad_down)
    grad_hidden, grad_bias_up = gelu_backward(hidden, grad_active, order, down_weight.shape[0])
    grad_second = dot(grad_hidden, w_up, ((1,), (1,)))
    shard_up = net.scatter_all(second, grad_hidden)
    upper = grad_second.astype(BF16)
    lower = (grad_second - upper.astype(F32)).astype(BF16)
    grad_second = dot(upper, shuffle, ((1,), (1,))) + dot(lower, shuffle, ((1,), (1,)))
    grad_gain_two = jnp.sum(grad_second * unit_two, 0)
    grad_shift_two = jnp.sum(grad_second, 0)
    grad_middle = dy + ln_back(unit_two, root_two, gains[2], grad_second)
    grad_gain_one = jnp.sum(grad_middle * unit_one, 0)
    grad_shift_one = jnp.sum(grad_middle, 0)
    grad_branch32 = ln_back(unit_one, root_one, gains[1], grad_middle)
    grad_bias_out = jnp.sum(grad_branch32, 0)
    grad_branch = grad_branch32.astype(BF16)
    grad_attended = dot(grad_branch, w_out, ((1,), (1,))).astype(BF16)
    shard_out = net.scatter_all(attended, grad_branch)
    grad_attended = dot(grad_attended, shuffle, ((1,), (1,))).astype(BF16)
    grad_attended = grad_attended.reshape(count, n_seq, lanes).transpose(1, 0, 2)
    grad_heads = swap_all(grad_attended, "seq").reshape(n_seq, MB, height, lanes)
    dq, dk, dv = attend_backward(
        pos, high, start, query, keys, values, grad_heads, turned, logsum, blk
    )
    grad_mixed = jnp.concatenate([dq, dk, dv], -1).reshape(n_seq * count, 3 * lanes)
    grad_bias_heads = jnp.sum(grad_mixed.astype(F32), 0)
    grad_normed = dot(grad_mixed, w_heads, ((1,), (1,))).reshape(n_seq, count, D)
    back = net.scatter_seq([grad_normed[j] for j in range(n_seq)])
    grad_gain_zero = sum(jnp.sum(grad_normed[j] * units[j], 0) for j in range(n_seq))
    grad_shift_zero = jnp.sum(grad_normed, (0, 1))
    unit_zero, root_zero = ln_stats(tokens)
    input_grad = (grad_middle + ln_back(unit_zero, root_zero, gains[0], back)).astype(BF16)

    term = dot(jnp.concatenate(normed, 0), grad_mixed, ((0,), (0,))).astype(BF16)
    term = swap_all(term.reshape(n_dp, n_seq * rows_qkv, 3 * lanes), "dp")
    term = jnp.sum(term.astype(F32), 0).astype(BF16)
    term = swap_all(term.reshape(n_seq, rows_qkv, 3 * lanes), "seq")
    term = term.reshape(n_seq, rows_qkv, 3, lanes).transpose(1, 2, 0, 3)
    shard_qkv = term.reshape(rows_qkv, 3 * D).astype(F32)

    def pack(vectors):
        many = len(vectors)
        return jnp.stack(vectors).reshape(many, devices, share).transpose(1, 0, 2).reshape(
            devices, many * share
        )

    grad_q = lax.dynamic_update_slice(jnp.zeros((D,), F32), grad_bias_heads[:lanes], (at,))
    grad_v = lax.dynamic_update_slice(jnp.zeros((D,), F32), grad_bias_heads[2 * lanes :], (at,))
    sums = jnp.concatenate(
        [
            pack([grad_q, grad_v, grad_bias_out, grad_bias_down]),
            grad_bias_up.reshape(devices, wide),
            pack([grad_gain_zero, grad_gain_one, grad_gain_two, grad_gain_three]),
            pack([grad_shift_zero, grad_shift_one, grad_shift_two, grad_shift_three]),
        ],
        1,
    )
    each = sums.shape[1]
    sums = sums.reshape(n_dp, n_seq, each).transpose(1, 0, 2).reshape(n_seq, n_dp * each)
    sums = jnp.sum(swap_all(sums, "seq"), 0).reshape(n_dp, each)
    sums = jnp.sum(swap_all(sums, "dp"), 0)
    first = 4 * share + wide

    return (
        layer_out.reshape(MB, 1, height, D),
        input_grad.reshape(MB, 1, height, D),
        shard_qkv,
        shard_out,
        shard_up,
        shard_down,
        sums[: 2 * share].reshape(2, share),
        sums[2 * share : 4 * share].reshape(2, share),
        sums[4 * share : first],
        sums[first : first + 4 * share].reshape(4, share),
        sums[first + 4 * share :].reshape(4, share),
    )


def solution(mesh):
    both = ("dp", "seq")
    in_specs = (
        P(None, "dp", "seq", None),
        P(None, "dp", "seq", None),
        P(None, "dp", None),
        P(both, None),
        P(both, None),
        P(both, None),
        P(both, None),
        P(None, both),
        P(None, both),
        P(both),
        P(None, both),
        P(None, both),
    )
    out_specs = (
        P(None, "dp", "seq", None),
        P(None, "dp", "seq", None),
        P(both, None),
        P(both, None),
        P(both, None),
        P(both, None),
        P(None, both),
        P(None, both),
        P(both),
        P(None, both),
        P(None, both),
    )
    step = functools.partial(body, mesh.shape["dp"], mesh.shape["seq"])
    return jax.shard_map(step, mesh=mesh, in_specs=in_specs, out_specs=out_specs, check_vma=False)
```
